512 devices in a mesh: vox: 32 (over z_lo, y), opt: 16 (over z_hi, x, core).
Axes of the slice: x: 4, y: 8, z: 8 (z_hi: 2, z_lo: 4; z = z_hi * 4 + z_lo), core: 2. Of those that a mesh axis runs over, the one named last changes fastest.
Arguments:
- source_fields: bfloat16 [1024, 24576], P('opt', 'vox'), may hold values from -6 to 6
- detector_fields: bfloat16 [4096, 24576], P('opt', 'vox'), may hold values from -6 to 6
- measured: float32 [1024, 4096], P('vox', 'opt'), may hold values from -6 to 6
- valid_pair: int32 [1024, 4096], P('vox', 'opt'), may hold values 0 or 1
- weight_class: int32 [1024, 4096], P('vox', 'opt'), may hold values from 0 to 3
- absorption: float32 [24576], P('vox'), may hold values from 0 to 1
Outputs:
- absorption_out: float32 [24576], P('vox')
- residual_out: float32 [1024, 4096], P('vox', 'opt')
The draws below stay inside these ranges and needn't reach their ends.
All inputs are finite; a program needn't handle non-finite values. No bound on the sum of `valid_pair` on one device may be relied on, other than what follows from the above.
Results may differ from the reference program's by a relative error of at most 0.0026.
Values may be sent and summed in bfloat16 or wider, within the bound.
No kernel may reach another device: no remote copies, remote signals or barrier semaphores. Data moves between devices by JAX's collectives and lax.ppermute only.
A program may use at most 64 MiB of HBM per device.

```python
import jax
import jax.numpy as jnp
from jax import lax

NS = 1024
ND = 4096
ITERS = 2
VOXELS = 24576


def place_ends(drawn, rng, least, top_value):
    dims = drawn.shape
    index_at = [jax.random.randint(jax.random.fold_in(rng, axis), (), 0, dims[axis]) for axis in range(len(dims))]
    drawn = drawn.at[tuple(index_at)].set(least)
    longest = dims.index(max(dims))
    index_at[longest] = (index_at[longest] + 1) % dims[longest]
    return drawn.at[tuple(index_at)].set(top_value)


def raised(array, own_key, source, target, parts, factor):
    def block_of(position):
        return (jnp.arange(array.shape[position]) // (array.shape[position] // parts)).reshape((-1,) + (1,) * (array.ndim - 1 - position))

    first = jax.random.permutation(own_key, parts)[block_of(target)]
    other_side = (block_of(target) + parts // 2) % parts
    return jnp.where((block_of(source) == first) | (block_of(source) == other_side), factor * array, array)


def levels(rng, extent, pieces, least, high):
    factor_of = 1.0
    for dim, parts in pieces:
        steps = jax.random.uniform(jax.random.fold_in(jax.random.fold_in(rng, 6), dim), (parts,), jnp.float32, least / len(pieces), high / len(pieces))
        factor_of = factor_of * jnp.repeat(jnp.exp(steps), extent[dim] // parts).reshape((-1,) + (1,) * (len(extent) - 1 - dim))
    return factor_of


def centred(stream_key, shape, deviation, bound, shards=(), kind=jnp.bfloat16):
    drawn = jax.random.normal(stream_key, shape, jnp.float32) * deviation
    if len(shards) > 0:
        drawn = levels(stream_key, shape, shards, -0.22, 0.18) * drawn
    return jnp.clip(drawn, min=-bound, max=bound).astype(kind)


def noise_with(rng, extent, spread, most, shards, heavy, held_as=jnp.bfloat16):
    entries = spread * jax.random.normal(rng, extent, jnp.float32)
    if shards:
        entries = entries * levels(rng, extent, shards, -0.22, 0.18)
    return jnp.clip(raised(entries, jax.random.fold_in(rng, 3), *heavy), -most, most).astype(held_as)


def setup_inputs(seed: int = 0) -> dict:
    seeds = jax.random.split(jax.random.key(seed), 7)
    source_fields = noise_with(seeds[0], (NS, VOXELS), 1.0, 6.0, ((0, 16), (1, 32)), (1, 0, 32, 2.75))
    detector_fields = centred(seeds[1], (ND, VOXELS), 1.0, 6.0, ((0, 16), (1, 32)))
    measured = centred(seeds[2], (NS, ND), 1.0, 6.0, ((0, 32), (1, 16)), jnp.float32)
    valid_pair = place_ends((jax.random.randint(seeds[3], (NS, ND), 0, 4) < 3).astype(jnp.int32), jax.random.fold_in(seeds[3], 1), 0, 1)
    weight_class = place_ends(jax.random.randint(seeds[4], (NS, ND), 0, 4), jax.random.fold_in(seeds[4], 1), 0, 3).astype(jnp.int32)
    absorption = jnp.clip(1.0 * jax.random.uniform(seeds[5], (VOXELS,), jnp.float32) ** levels(seeds[5], (VOXELS,), ((0, 32),), -0.2, 0.2), 0.0, 1.0)
    return dict(source_fields=source_fields, detector_fields=detector_fields, measured=measured, valid_pair=valid_pair, weight_class=weight_class, absorption=absorption)


def reference(source_fields, detector_fields, measured, valid_pair, weight_class, absorption):
    voxels = source_fields.shape[1]
    pred_scale = 1.0 / jnp.sqrt(jnp.float32(voxels))
    grad_scale = jnp.sqrt(jnp.float32(voxels)) / (jnp.float32(NS) * jnp.float32(ND))
    maskf = valid_pair.astype(jnp.float32) / (1.0 + weight_class.astype(jnp.float32))
    mu_now = absorption
    weighted = jnp.zeros(measured.shape, jnp.float32)
    for step in range(ITERS):
        scaled = (detector_fields.astype(jnp.float32) * mu_now[None, :]).astype(jnp.bfloat16)
        predicted = lax.dot_general(source_fields, scaled, (((1,), (1,)), ((), ())), preferred_element_type=jnp.float32) * pred_scale
        weighted = maskf * (predicted - measured)
        weighted_b = weighted.astype(jnp.bfloat16)
        inner = jnp.dot(weighted_b, detector_fields, preferred_element_type=jnp.float32)
        gradient = lax.optimization_barrier(jnp.sum(inner * source_fields.astype(jnp.float32), axis=0)) * grad_scale
        mu_now = jnp.maximum(mu_now - 2.0 * gradient, 0.0)
    return (mu_now, weighted)
```

```python
import jax
import jax.numpy as jnp
from jax import lax
from jax.sharding import Mesh
from jax.sharding import PartitionSpec as P

NS = 1024
ND = 4096
ITERS = 2
VOX = ("z_lo", "y")
OPT = ("z_hi", "x", "core")


def everywhere(block, axes, count):
    return lax.all_to_all(jnp.broadcast_to(block[None], (count,) + block.shape), axes, 0, 0)


def gather_sources(rows):
    own, cols = rows.shape
    swapped = lax.ppermute(rows, "z_hi", [(0, 1), (1, 0)])
    low = lax.axis_index("z_hi") == 0
    both = jnp.concatenate([jnp.where(low, rows, swapped), jnp.where(low, swapped, rows)], axis=0)
    along = lax.all_gather(both, "x", axis=0)
    along = along.reshape(4, 2, own, cols)
    parts = []
    for z in range(2):
        half = lax.all_gather(along[:, z], "core", axis=1)
        parts.append(half)
    return jnp.stack(parts).reshape(16 * own, cols)


def local(source_fields, detector_fields, measured, valid_pair, weight_class, absorption):
    voxels = absorption.shape[0] * 32
    pred_scale = 1.0 / jnp.sqrt(jnp.float32(voxels))
    grad_scale = jnp.sqrt(jnp.float32(voxels)) / (jnp.float32(NS) * jnp.float32(ND))
    own_rows, own_cols = measured.shape
    maskf = valid_pair.astype(jnp.float32) / (1.0 + weight_class.astype(jnp.float32))
    sources = gather_sources(source_fields)
    mu_now = absorption
    weighted = None
    for step in range(ITERS):
        scaled = (detector_fields * mu_now[None, :]).astype(jnp.bfloat16)
        partial_pred = lax.dot_general(
            sources, scaled, (((1,), (1,)), ((), ())), preferred_element_type=jnp.float32
        )
        sent = partial_pred.astype(jnp.bfloat16).reshape(32, own_rows, own_cols)
        got = lax.all_to_all(sent, VOX, 0, 0)
        predicted = jnp.sum(got.astype(jnp.float32), axis=0)
        weighted = maskf * (predicted * pred_scale - measured)
        weighted_b = weighted.astype(jnp.bfloat16)
        all_weighted = everywhere(weighted_b, VOX, 32).reshape(32 * own_rows, own_cols)
        inner = jnp.dot(all_weighted, detector_fields, preferred_element_type=jnp.float32)
        local_grad = jnp.sum(inner * sources, axis=0)
        terms = everywhere(local_grad.reshape(6, 128), OPT, 16)
        gradient = jnp.sum(terms, axis=0).reshape(-1) * grad_scale
        mu_now = jnp.maximum(mu_now - 2.0 * gradient, 0.0)
    return (mu_now, weighted)


def solution(mesh):
    names = ("z_lo", "y", "z_hi", "x", "core")
    fine = Mesh(mesh.devices.reshape(4, 8, 2, 4, 2), names)
    placed = (P(OPT, VOX), P(OPT, VOX), P(VOX, OPT), P(VOX, OPT), P(VOX, OPT), P(VOX))
    return jax.shard_map(
        local, mesh=fine, in_specs=placed, out_specs=(P(VOX), P(VOX, OPT)), check_vma=False
    )
```

```python
import jax
import jax.numpy as jnp
from jax import lax
from jax.sharding import Mesh
from jax.sharding import PartitionSpec as P

NS = 1024
ND = 4096
ITERS = 2
AXES = ("z_lo", "y", "z_hi", "x", "core")
VOX = ("z_lo", "y")
OPT = ("z_hi", "x", "core")
BF16 = jnp.bfloat16


def everywhere(block, axes, count):
    return lax.all_to_all(jnp.broadcast_to(block[None], (count,) + block.shape), axes, 0, 0)


def pair_moves():
    moves = []
    for k in range(4):
        for y in range(8):
            for z in range(2):
                for x in range(4):
                    for c in range(2):
                        k_new = x
                        x_new = (k % 2) * 2 + y // 4
                        y_new = ((k // 2) ^ z) * 4 + (((y // 2) % 2) ^ c) * 2 + y % 2
                        here = (((k * 8 + y) * 2 + z) * 4 + x) * 2 + c
                        there = (((k_new * 8 + y_new) * 2 + z) * 4 + x_new) * 2 + c
                        moves.append((here, there))
    return moves


def three_parts(values):
    high = lax.reduce_precision(values, 8, 7)
    rest = values - high
    middle = lax.reduce_precision(rest, 8, 7)
    return [high, middle, rest - middle]


def local(source_fields, detector_fields, measured, valid_pair, weight_class, absorption):
    cols = absorption.shape[0]
    rows = source_fields.shape[0]
    voxels = cols * 32
    own_rows, own_cols = measured.shape
    pred_scale = 1.0 / jnp.sqrt(jnp.float32(voxels))
    grad_scale = jnp.sqrt(jnp.float32(voxels)) / (jnp.float32(NS) * jnp.float32(ND))
    moves = pair_moves()
    x_now = lax.axis_index("x")

    turned = lax.ppermute(
        detector_fields, ("z_lo", "x"), [(k * 4 + x, x * 4 + k) for k in range(4) for x in range(4)]
    )
    other_z = lax.ppermute(source_fields, "z_hi", [(0, 1), (1, 0)])

    maskf = valid_pair.astype(jnp.float32) / (1.0 + weight_class.astype(jnp.float32))
    pairs = lax.ppermute(jnp.concatenate([measured, maskf], axis=0), AXES, moves)
    measured, maskf = pairs[:own_rows], pairs[own_rows:]

    shifted = [turned] + [
        lax.ppermute(turned, "x", [((x + step) % 4, x) for x in range(4)]) for step in (1, 2, 3)
    ]

    parts = jnp.stack(three_parts(absorption)).astype(BF16)
    parts = jnp.concatenate([parts, jnp.zeros((13, cols), BF16)], axis=0)
    along = lax.all_gather(
        jnp.concatenate([source_fields, other_z, parts], axis=0), "z_lo", axis=0
    )
    mine = along[:, : 2 * rows]
    other_core = lax.ppermute(mine, "core", [(0, 1), (1, 0)])
    sources = jnp.concatenate(
        [mine[:, :rows], other_core[:, :rows], mine[:, rows:], other_core[:, rows:]], axis=1
    )
    mu_parts = along[:, 2 * rows : 2 * rows + 3].astype(jnp.float32)
    mu_now = (mu_parts[:, 0] + mu_parts[:, 1]) + mu_parts[:, 2]

    detectors = jnp.zeros((4,) + detector_fields.shape, BF16)
    for step, block in enumerate(shifted):
        detectors = lax.dynamic_update_slice_in_dim(
            detectors, block[None], lax.rem(x_now + step, 4), 0
        )

    weighted = None
    for step in range(ITERS):
        scaled = (detectors * mu_now[:, None, :]).astype(BF16)
        partial_pred = lax.dot_general(
            sources, scaled, (((0, 2), (0, 2)), ((), ())), preferred_element_type=jnp.float32
        )
        sent = partial_pred.astype(BF16).reshape(8, own_rows, own_cols)
        got = lax.all_to_all(sent, "y", 0, 0)
        predicted = jnp.sum(got.astype(jnp.float32), axis=0)
        weighted = maskf * (predicted * pred_scale - measured)
        weighted_b = weighted.astype(BF16)
        all_weighted = everywhere(weighted_b, "y", 8).reshape(8 * own_rows, own_cols)
        local_grad = jnp.concatenate(
            [
                jnp.sum(
                    jnp.dot(all_weighted, detectors[k], preferred_element_type=jnp.float32)
                    * sources[k],
                    axis=0,
                ).reshape(cols // 128, 128)
                for k in range(4)
            ],
            axis=0,
        )
        total = jnp.sum(lax.all_gather(local_grad, "core", axis=0), axis=0)
        total = jnp.sum(everywhere(total, "x", 4), axis=0)
        total = jnp.sum(everywhere(total, ("z_lo", "z_hi"), 8), axis=0)
        gradient = total.reshape(4, cols) * grad_scale
        mu_now = jnp.maximum(mu_now - 2.0 * gradient, 0.0)
    back = lax.ppermute(weighted, AXES, [(there, here) for here, there in moves])
    own_mu = lax.dynamic_index_in_dim(mu_now, lax.axis_index("z_lo"), 0, keepdims=False)
    return (own_mu, back)


def solution(mesh):
    fine = Mesh(mesh.devices.reshape(4, 8, 2, 4, 2), AXES)
    placed = (P(OPT, VOX), P(OPT, VOX), P(VOX, OPT), P(VOX, OPT), P(VOX, OPT), P(VOX))
    return jax.shard_map(
        local, mesh=fine, in_specs=placed, out_specs=(P(VOX), P(VOX, OPT)), check_vma=False
    )
```

```python
import jax
import jax.numpy as jnp
from jax import lax
from jax.sharding import Mesh
from jax.sharding import PartitionSpec as P

NS = 1024
ND = 4096
ITERS = 2
AXES = ("z_lo", "y_hi", "y_lo", "z_hi", "x", "core")
VOX = ("z_lo", "y_hi", "y_lo")
OPT = ("z_hi", "x", "core")
SUM = ("z_lo", "y_hi")
REST = ("y_lo", "z_hi", "x")
BF16 = jnp.bfloat16
SWAP = [(0, 1), (1, 0)]


def everywhere(block, axes, count):
    return lax.all_to_all(jnp.broadcast_to(block[None], (count,) + block.shape), axes, 0, 0)


def ordered(first, own, other):
    return jnp.where(first, own, other), jnp.where(first, other, own)


def gather_sources(block, low_y):
    half = block.shape[0] // 2
    cols = block.shape[1]
    sent = jnp.broadcast_to(block.reshape(2, 1, half, cols), (2, 2, half, cols))
    got = lax.all_to_all(sent.reshape(4, half, cols), ("y_lo", "z_hi"), 0, 0)
    got = got.reshape(2, 2, half, cols)
    pieces = jnp.concatenate(ordered(low_y, got[0], got[1]), axis=2)
    along = lax.all_gather(pieces, "x", axis=0)
    both = [lax.all_gather(along[:, z], "core", axis=1) for z in range(2)]
    return jnp.stack(both).reshape(16 * half, 2 * cols)


def local(source_fields, detector_fields, measured, valid_pair, weight_class, absorption):
    cols = absorption.shape[0]
    voxels = cols * 32
    own_rows, own_cols = measured.shape
    pred_scale = 1.0 / jnp.sqrt(jnp.float32(voxels))
    grad_scale = jnp.sqrt(jnp.float32(voxels)) / (jnp.float32(NS) * jnp.float32(ND))
    low_y = lax.axis_index("y_lo") == 0
    maskf = valid_pair.astype(jnp.float32) / (1.0 + weight_class.astype(jnp.float32))

    sources = gather_sources(source_fields, low_y)
    source_cols = [sources[:, :cols], sources[:, cols:]]
    detectors = [detector_fields, lax.ppermute(detector_fields, "y_lo", SWAP)]
    mu_now = [absorption, lax.ppermute(absorption, "y_lo", SWAP)]

    weighted = None
    for step in range(ITERS):
        partial_pred = 0.0
        for s, d, mu in zip(source_cols, detectors, mu_now):
            scaled = (d * mu[None, :]).astype(BF16)
            partial_pred = partial_pred + lax.dot_general(
                s, scaled, (((1,), (1,)), ((), ())), preferred_element_type=jnp.float32
            )
        sent = partial_pred.astype(BF16).reshape(16, own_rows, own_cols)
        got = lax.all_to_all(sent, SUM, 0, 0)
        predicted = jnp.sum(got.astype(jnp.float32), axis=0)
        weighted = maskf * (predicted * pred_scale - measured)
        weighted_b = weighted.astype(BF16)
        all_weighted = everywhere(weighted_b, SUM, 16).reshape(16 * own_rows, own_cols)
        terms = [
            jnp.sum(jnp.dot(all_weighted, d, preferred_element_type=jnp.float32) * s, axis=0)
            for s, d in zip(source_cols, detectors)
        ]
        terms = jnp.stack(ordered(low_y, *terms)).reshape(2 * cols // 128, 128)
        total = jnp.sum(lax.all_gather(terms, "core", axis=0), axis=0)
        total = jnp.sum(everywhere(total, REST, 16), axis=0).reshape(2, cols)
        gradient = [g * grad_scale for g in ordered(low_y, total[0], total[1])]
        mu_now = [jnp.maximum(mu - 2.0 * g, 0.0) for mu, g in zip(mu_now, gradient)]
    return (mu_now[0], weighted)


def solution(mesh):
    fine = Mesh(mesh.devices.reshape(4, 4, 2, 2, 4, 2), AXES)
    placed = (P(OPT, VOX), P(OPT, VOX), P(VOX, OPT), P(VOX, OPT), P(VOX, OPT), P(VOX))
    return jax.shard_map(
        local, mesh=fine, in_specs=placed, out_specs=(P(VOX), P(VOX, OPT)), check_vma=False
    )
```

```python
import jax
import jax.numpy as jnp
from jax import lax
from jax.sharding import Mesh
from jax.sharding import PartitionSpec as P

NS = 1024
ND = 4096
ITERS = 2
AXES = ("z_mid", "z_low", "y", "z_hi", "x", "core")
VOX = ("z_mid", "z_low", "y")
OPT = ("z_hi", "x", "core")
SUM = ("z_low", "y")
REST = ("z_mid", "z_hi", "x")
BF16 = jnp.bfloat16
SWAP = [(0, 1), (1, 0)]


def everywhere(block, axes, count):
    return lax.all_to_all(jnp.broadcast_to(block[None], (count,) + block.shape), axes, 0, 0)


def ordered(first, own, other):
    return jnp.where(first, own, other), jnp.where(first, other, own)


def gather_sources(block, aligned):
    rows, cols = block.shape
    first = lax.ppermute(block, ("z_mid", "z_hi"), [(0, 0), (1, 2), (2, 1), (3, 3)])
    second = lax.ppermute(block, ("z_mid", "z_hi"), [(0, 1), (1, 3), (2, 0), (3, 2)])
    along = everywhere(jnp.stack(ordered(aligned, first, second)), "x", 4)
    return [
        lax.all_gather(along[:, k], "core", axis=1).reshape(8 * rows, cols) for k in range(2)
    ]


def local(source_fields, detector_fields, measured, valid_pair, weight_class, absorption):
    cols = absorption.shape[0]
    voxels = cols * 32
    own_rows, own_cols = measured.shape
    pred_scale = 1.0 / jnp.sqrt(jnp.float32(voxels))
    grad_scale = jnp.sqrt(jnp.float32(voxels)) / (jnp.float32(NS) * jnp.float32(ND))
    low = lax.axis_index("z_mid") == 0
    maskf = valid_pair.astype(jnp.float32) / (1.0 + weight_class.astype(jnp.float32))

    sources = gather_sources(source_fields, lax.axis_index("z_mid") == lax.axis_index("z_hi"))
    detectors = [detector_fields, lax.ppermute(detector_fields, "z_mid", SWAP)]
    mu_now = [absorption, lax.ppermute(absorption, "z_mid", SWAP)]

    weighted = None
    for step in range(ITERS):
        partial_pred = 0.0
        for s, d, mu in zip(sources, detectors, mu_now):
            scaled = (d * mu[None, :]).astype(BF16)
            partial_pred = partial_pred + lax.dot_general(
                s, scaled, (((1,), (1,)), ((), ())), preferred_element_type=jnp.float32
            )
        sent = partial_pred.astype(BF16).reshape(16, own_rows, own_cols)
        got = lax.all_to_all(sent, SUM, 0, 0)
        predicted = jnp.sum(got.astype(jnp.float32), axis=0)
        weighted = maskf * (predicted * pred_scale - measured)
        weighted_b = weighted.astype(BF16)
        all_weighted = everywhere(weighted_b, SUM, 16).reshape(16 * own_rows, own_cols)
        terms = [
            jnp.sum(jnp.dot(all_weighted, d, preferred_element_type=jnp.float32) * s, axis=0)
            for s, d in zip(sources, detectors)
        ]
        terms = jnp.stack(ordered(low, *terms)).reshape(2 * cols // 128, 128)
        total = jnp.sum(lax.all_gather(terms, "core", axis=0), axis=0)
        total = jnp.sum(everywhere(total, REST, 16), axis=0).reshape(2, cols)
        gradient = [g * grad_scale for g in ordered(low, total[0], total[1])]
        mu_now = [jnp.maximum(mu - 2.0 * g, 0.0) for mu, g in zip(mu_now, gradient)]
    return (mu_now[0], weighted)


def solution(mesh):
    fine = Mesh(mesh.devices.reshape(2, 2, 8, 2, 4, 2), AXES)
    placed = (P(OPT, VOX), P(OPT, VOX), P(VOX, OPT), P(VOX, OPT), P(VOX, OPT), P(VOX))
    return jax.shard_map(
        local, mesh=fine, in_specs=placed, out_specs=(P(VOX), P(VOX, OPT)), check_vma=False
    )
```

```python
import jax
import jax.numpy as jnp
from jax import lax
from jax.sharding import Mesh
from jax.sharding import PartitionSpec as P


NS = 1024
ND = 4096
ITERS = 2
AXES = ("z_mid", "z_low", "y", "z_hi", "x", "core")
VOX = ("z_mid", "z_low", "y")
OPT = ("z_hi", "x", "core")
SUM = ("z_low", "y")
REST = ("z_mid", "z_hi", "x")
BF16 = jnp.bfloat16
SWAP = [(0, 1), (1, 0)]


def everywhere(block, axes, count):
    return lax.all_to_all(jnp.broadcast_to(block[None], (count,) + block.shape), axes, 0, 0)


def ordered(first, own, other):
    return jnp.where(first, own, other), jnp.where(first, other, own)


def gather_sources(block, aligned):
    rows, cols = block.shape
    first = lax.ppermute(block, ("z_mid", "z_hi"), [(0, 0), (1, 2), (2, 1), (3, 3)])
    second = lax.ppermute(block, ("z_mid", "z_hi"), [(0, 1), (1, 3), (2, 0), (3, 2)])
    pieces = jnp.stack(ordered(aligned, first, second))
    along = everywhere(pieces, "x", 4)
    return [
        lax.all_gather(along[:, k], "core", axis=1).reshape(8 * rows, cols) for k in range(2)
    ]


def local(source_fields, detector_fields, measured, valid_pair, weight_class, absorption):
    cols = absorption.shape[0]
    voxels = cols * 32
    own_rows, own_cols = measured.shape
    pred_scale = 1.0 / jnp.sqrt(jnp.float32(voxels))
    grad_scale = jnp.sqrt(jnp.float32(voxels)) / (jnp.float32(NS) * jnp.float32(ND))
    low = lax.axis_index("z_mid") == 0
    maskf = valid_pair.astype(jnp.float32) / (1.0 + weight_class.astype(jnp.float32))

    sources = gather_sources(source_fields, lax.axis_index("z_mid") == lax.axis_index("z_hi"))
    detectors = [detector_fields, lax.ppermute(detector_fields, "z_mid", SWAP)]
    mu_now = [absorption, lax.ppermute(absorption, "z_mid", SWAP)]

    weighted = None
    for _ in range(ITERS):
        partial_pred = 0.0
        for s, d, mu in zip(sources, detectors, mu_now):
            scaled = (d * mu[None, :]).astype(BF16)
            partial_pred = partial_pred + lax.dot_general(
                s, scaled, (((1,), (1,)), ((), ())), preferred_element_type=jnp.float32
            )
        sent = partial_pred.astype(BF16).reshape(16, own_rows, own_cols)
        got = lax.all_to_all(sent, SUM, 0, 0)
        predicted = jnp.sum(got.astype(jnp.float32), axis=0)
        weighted = maskf * (predicted * pred_scale - measured)
        weighted_b = weighted.astype(BF16)
        all_weighted = everywhere(weighted_b, SUM, 16).reshape(16 * own_rows, own_cols)
        terms = [
            jnp.sum(jnp.dot(all_weighted, d, preferred_element_type=jnp.float32) * s, axis=0)
            for s, d in zip(sources, detectors)
        ]
        terms = jnp.stack(ordered(low, *terms)).reshape(2 * cols // 128, 128)
        total = jnp.sum(lax.all_gather(terms, "core", axis=0), axis=0)
        total = jnp.sum(everywhere(total, REST, 16), axis=0).reshape(2, cols)
        gradient = [g * grad_scale for g in ordered(low, total[0], total[1])]
        mu_now = [jnp.maximum(mu - 2.0 * g, 0.0) for mu, g in zip(mu_now, gradient)]
    return (mu_now[0], weighted)


def solution(mesh):
    fine = Mesh(mesh.devices.reshape(2, 2, 8, 2, 4, 2), AXES)
    placed = (P(OPT, VOX), P(OPT, VOX), P(VOX, OPT), P(VOX, OPT), P(VOX, OPT), P(VOX))
    return jax.shard_map(
        local, mesh=fine, in_specs=placed, out_specs=(P(VOX), P(VOX, OPT)), check_vma=False
    )
```

```python
import jax
import jax.numpy as jnp
from jax import lax
from jax.sharding import Mesh
from jax.sharding import PartitionSpec as P


NS = 1024
ND = 4096
ITERS = 2
AXES = ("z_mid", "z_low", "y", "z_hi", "x", "core")
VOX = ("z_mid", "z_low", "y")
OPT = ("z_hi", "x", "core")
SUM = ("z_low", "y")
REST = ("z_mid", "z_hi", "x")
BF16 = jnp.bfloat16
SWAP = [(0, 1), (1, 0)]


def everywhere(block, axes, count):
    return lax.all_to_all(jnp.broadcast_to(block[None], (count,) + block.shape), axes, 0, 0)


def ordered(first, own, other):
    return jnp.where(first, own, other), jnp.where(first, other, own)


def gather_sources(block, aligned):
    rows, cols = block.shape
    first = lax.ppermute(block, ("z_mid", "z_hi"), [(0, 0), (1, 2), (2, 1), (3, 3)])
    second = lax.ppermute(block, ("z_mid", "z_hi"), [(0, 1), (1, 3), (2, 0), (3, 2)])
    pieces = jnp.stack(ordered(aligned, first, second))
    along = everywhere(pieces, "x", 4)
    return [
        lax.all_gather(along[:, k], "core", axis=1).reshape(8 * rows, cols) for k in range(2)
    ]


def local(source_fields, detector_fields, measured, valid_pair, weight_class, absorption):
    cols = absorption.shape[0]
    voxels = cols * 32
    own_rows, own_cols = measured.shape
    pred_scale = 1.0 / jnp.sqrt(jnp.float32(voxels))
    grad_scale = jnp.sqrt(jnp.float32(voxels)) / (jnp.float32(NS) * jnp.float32(ND))
    low = lax.axis_index("z_mid") == 0
    maskf = valid_pair.astype(jnp.float32) / (1.0 + weight_class.astype(jnp.float32))

    sources = gather_sources(source_fields, lax.axis_index("z_mid") == lax.axis_index("z_hi"))
    detectors = [detector_fields, lax.ppermute(detector_fields, "z_mid", SWAP)]
    mu_now = [absorption, lax.ppermute(absorption, "z_mid", SWAP)]

    weighted = None
    for step in range(ITERS):
        partial_pred = 0.0
        for s, d, mu in zip(sources, detectors, mu_now):
            scaled = (d * mu[None, :]).astype(BF16)
            partial_pred = partial_pred + lax.dot_general(
                s, scaled, (((1,), (1,)), ((), ())), preferred_element_type=jnp.float32
            )
        sent = partial_pred.astype(BF16).reshape(16, own_rows, own_cols)
        got = lax.all_to_all(sent, SUM, 0, 0)
        predicted = jnp.sum(got.astype(jnp.float32), axis=0)
        weighted = maskf * (predicted * pred_scale - measured)
        weighted_b = weighted.astype(BF16)
        all_weighted = everywhere(weighted_b, SUM, 16).reshape(16 * own_rows, own_cols)
        terms = [
            jnp.sum(jnp.dot(all_weighted, d, preferred_element_type=jnp.float32) * s, axis=0)
            for s, d in zip(sources, detectors)
        ]
        terms = jnp.stack(ordered(low, *terms)).reshape(2 * cols // 128, 128)
        total = jnp.sum(lax.all_gather(terms, "core", axis=0), axis=0)
        if step < ITERS - 1:
            total = jnp.sum(everywhere(total, REST, 16), axis=0).reshape(2, cols)
            gradient = ordered(low, total[0], total[1])
        else:
            total = jnp.broadcast_to(total.reshape(2, 1, -1, 128), (2, 8, cols // 128, 128))
            total = lax.all_to_all(total.reshape(16, cols // 128, 128), REST, 0, 0)
            gradient = [jnp.sum(total, axis=0).reshape(cols)]
        mu_now = [jnp.maximum(mu - 2.0 * (g * grad_scale), 0.0) for mu, g in zip(mu_now, gradient)]
    return (mu_now[0], weighted)


def solution(mesh):
    fine = Mesh(mesh.devices.reshape(2, 2, 8, 2, 4, 2), AXES)
    placed = (P(OPT, VOX), P(OPT, VOX), P(VOX, OPT), P(VOX, OPT), P(VOX, OPT), P(VOX))
    return jax.shard_map(
        local, mesh=fine, in_specs=placed, out_specs=(P(VOX), P(VOX, OPT)), check_vma=False
    )
```

```python
import jax
import jax.numpy as jnp
from jax import lax
from jax.sharding import Mesh
from jax.sharding import PartitionSpec as P


NS = 1024
ND = 4096
ITERS = 2
AXES = ("z_mid", "z_low", "y", "z_hi", "x", "core")
VOX = ("z_mid", "z_low", "y")
OPT = ("z_hi", "x", "core")
SUM = ("z_low", "y")
REST = ("z_mid", "z_hi", "x")
BF16 = jnp.bfloat16
SWAP = [(0, 1), (1, 0)]


def everywhere(block, axes, count):
    return lax.all_to_all(jnp.broadcast_to(block[None], (count,) + block.shape), axes, 0, 0)


def ordered(first, own, other):
    return jnp.where(first, own, other), jnp.where(first, other, own)


def gather_sources(block, aligned, low):
    rows, cols = block.shape
    first = lax.ppermute(block, ("z_mid", "z_hi"), [(0, 0), (1, 2), (2, 1), (3, 3)])
    second = lax.ppermute(block, ("z_mid", "z_hi"), [(0, 1), (1, 3), (2, 0), (3, 2)])
    pieces = jnp.stack(ordered(aligned, first, second))
    pieces, low = lax.optimization_barrier((pieces, low))
    along = everywhere(pieces, "x", 4)
    gathered = [
        lax.all_gather(along[:, k], "core", axis=1).reshape(8 * rows, cols) for k in range(2)
    ]
    return gathered, low


def local(source_fields, detector_fields, measured, valid_pair, weight_class, absorption):
    cols = absorption.shape[0]
    voxels = cols * 32
    own_rows, own_cols = measured.shape
    pred_scale = 1.0 / jnp.sqrt(jnp.float32(voxels))
    grad_scale = jnp.sqrt(jnp.float32(voxels)) / (jnp.float32(NS) * jnp.float32(ND))
    maskf = valid_pair.astype(jnp.float32) / (1.0 + weight_class.astype(jnp.float32))

    aligned = lax.axis_index("z_mid") == lax.axis_index("z_hi")
    sources, low = gather_sources(source_fields, aligned, lax.axis_index("z_mid") == 0)
    detectors = [detector_fields, lax.ppermute(detector_fields, "z_mid", SWAP)]
    mu_now = [absorption, lax.ppermute(absorption, "z_mid", SWAP)]

    weighted = None
    for step in range(ITERS):
        partial_pred = 0.0
        for s, d, mu in zip(sources, detectors, mu_now):
            scaled = (d * mu[None, :]).astype(BF16)
            partial_pred = partial_pred + lax.dot_general(
                s, scaled, (((1,), (1,)), ((), ())), preferred_element_type=jnp.float32
            )
        sent = partial_pred.astype(BF16).reshape(16, own_rows, own_cols)
        got = lax.all_to_all(sent, SUM, 0, 0)
        predicted = jnp.sum(got.astype(jnp.float32), axis=0)
        weighted = maskf * (predicted * pred_scale - measured)
        weighted_b = weighted.astype(BF16)
        all_weighted = everywhere(weighted_b, SUM, 16).reshape(16 * own_rows, own_cols)
        terms = [
            jnp.sum(jnp.dot(all_weighted, d, preferred_element_type=jnp.float32) * s, axis=0)
            for s, d in zip(sources, detectors)
        ]
        terms = jnp.stack(ordered(low, *terms)).reshape(2 * cols // 128, 128)
        total = jnp.sum(lax.all_gather(terms, "core", axis=0), axis=0)
        if step < ITERS - 1:
            total = jnp.sum(everywhere(total, REST, 16), axis=0).reshape(2, cols)
            gradient = ordered(low, total[0], total[1])
        else:
            total = jnp.broadcast_to(total.reshape(2, 1, -1, 128), (2, 8, cols // 128, 128))
            total = lax.all_to_all(total.reshape(16, cols // 128, 128), REST, 0, 0)
            gradient = [jnp.sum(total, axis=0).reshape(cols)]
        mu_now = [jnp.maximum(mu - 2.0 * (g * grad_scale), 0.0) for mu, g in zip(mu_now, gradient)]
    return (mu_now[0], weighted)


def solution(mesh):
    fine = Mesh(mesh.devices.reshape(2, 2, 8, 2, 4, 2), AXES)
    placed = (P(OPT, VOX), P(OPT, VOX), P(VOX, OPT), P(VOX, OPT), P(VOX, OPT), P(VOX))
    return jax.shard_map(
        local, mesh=fine, in_specs=placed, out_specs=(P(VOX), P(VOX, OPT)), check_vma=False
    )
```

```python
import jax
import jax.numpy as jnp
from jax import lax
from jax.sharding import Mesh
from jax.sharding import PartitionSpec as P


NS = 1024
ND = 4096
ITERS = 2
AXES = ("z_mid", "z_low", "y", "z_hi", "x", "core")
VOX = ("z_mid", "z_low", "y")
OPT = ("z_hi", "x", "core")
SUM = ("z_low", "y")
REST = ("z_mid", "z_hi", "x")
BF16 = jnp.bfloat16
SWAP = [(0, 1), (1, 0)]


def everywhere(block, axes, count):
    return lax.all_to_all(jnp.broadcast_to(block[None], (count,) + block.shape), axes, 0, 0)


def ordered(first, own, other):
    return jnp.where(first, own, other), jnp.where(first, other, own)


def gather_sources(block, aligned, low):
    rows, cols = block.shape
    first = lax.ppermute(block, ("z_mid", "z_hi"), [(0, 0), (1, 2), (2, 1), (3, 3)])
    second = lax.ppermute(block, ("z_mid", "z_hi"), [(0, 1), (1, 3), (2, 0), (3, 2)])
    pieces = jnp.stack(ordered(aligned, first, second))
    pieces, low = lax.optimization_barrier((pieces, low))
    along = everywhere(pieces, "x", 4)
    gathered = [
        lax.all_gather(along[:, k], "core", axis=1).reshape(8 * rows, cols) for k in range(2)
    ]
    return gathered, low


def local(source_fields, detector_fields, measured, valid_pair, weight_class, absorption):
    cols = absorption.shape[0]
    voxels = cols * 32
    own_rows, own_cols = measured.shape
    pred_scale = 1.0 / jnp.sqrt(jnp.float32(voxels))
    grad_scale = jnp.sqrt(jnp.float32(voxels)) / (jnp.float32(NS) * jnp.float32(ND))
    maskf = valid_pair.astype(jnp.float32) / (1.0 + weight_class.astype(jnp.float32))

    aligned = lax.axis_index("z_mid") == lax.axis_index("z_hi")
    sources, low = gather_sources(source_fields, aligned, lax.axis_index("z_mid") == 0)
    detectors = [detector_fields, lax.ppermute(detector_fields, "z_mid", SWAP)]
    mu_now = [absorption, lax.ppermute(absorption, "z_mid", SWAP)]

    weighted = None
    for step in range(ITERS):
        partial_pred = 0.0
        for s, d, mu in zip(sources, detectors, mu_now):
            scaled = (d * mu[None, :]).astype(BF16)
            partial_pred = partial_pred + lax.dot_general(
                s, scaled, (((1,), (1,)), ((), ())), preferred_element_type=jnp.float32
            )
        sent = partial_pred.astype(BF16).reshape(16, own_rows, own_cols)
        got = lax.all_to_all(sent, SUM, 0, 0)
        predicted = jnp.sum(got.astype(jnp.float32), axis=0)
        weighted = maskf * (predicted * pred_scale - measured)
        weighted_b = weighted.astype(BF16)
        all_weighted = everywhere(weighted_b, SUM, 16).reshape(16 * own_rows, own_cols)
        terms = [
            jnp.sum(jnp.dot(all_weighted, d, preferred_element_type=jnp.float32) * s, axis=0)
            for s, d in zip(sources, detectors)
        ]
        terms = jnp.stack(ordered(low, *terms)).reshape(1, 2 * cols)
        total = jnp.sum(lax.all_gather(terms, "core", axis=0), axis=0)
        if step < ITERS - 1:
            total = jnp.sum(everywhere(total, REST, 16), axis=0).reshape(2, cols)
            gradient = ordered(low, total[0], total[1])
        else:
            total = jnp.broadcast_to(total.reshape(2, 1, cols), (2, 8, cols))
            total = lax.all_to_all(total.reshape(16, 1, cols), REST, 0, 0)
            gradient = [jnp.sum(total, axis=0).reshape(cols)]
        mu_now = [jnp.maximum(mu - 2.0 * (g * grad_scale), 0.0) for mu, g in zip(mu_now, gradient)]
    return (mu_now[0], weighted)


def solution(mesh):
    fine = Mesh(mesh.devices.reshape(2, 2, 8, 2, 4, 2), AXES)
    placed = (P(OPT, VOX), P(OPT, VOX), P(VOX, OPT), P(VOX, OPT), P(VOX, OPT), P(VOX))
    return jax.shard_map(
        local, mesh=fine, in_specs=placed, out_specs=(P(VOX), P(VOX, OPT)), check_vma=False
    )
```

```python
import jax
import jax.numpy as jnp
from jax import lax
from jax.sharding import Mesh
from jax.sharding import PartitionSpec as P


NS = 1024
ND = 4096
ITERS = 2
AXES = ("z_mid", "z_low", "y", "z_hi", "x", "core")
VOX = ("z_mid", "z_low", "y")
OPT = ("z_hi", "x", "core")
SUM = ("z_low", "y")
REST = ("z_mid", "z_hi", "x")
BF16 = jnp.bfloat16
SWAP = [(0, 1), (1, 0)]


def everywhere(block, axes, count):
    return lax.all_to_all(jnp.broadcast_to(block[None], (count,) + block.shape), axes, 0, 0)


def ordered(first, own, other):
    return jnp.where(first, own, other), jnp.where(first, other, own)


def gather_sources(block, aligned, low):
    rows, cols = block.shape
    first = lax.ppermute(block, ("z_mid", "z_hi"), [(0, 0), (1, 2), (2, 1), (3, 3)])
    second = lax.ppermute(block, ("z_mid", "z_hi"), [(0, 1), (1, 3), (2, 0), (3, 2)])
    pieces = jnp.stack(ordered(aligned, first, second))
    pieces, low = lax.optimization_barrier((pieces, low))
    along = everywhere(pieces, "x", 4)
    gathered = [
        lax.all_gather(along[:, k], "core", axis=1).reshape(8 * rows, cols) for k in range(2)
    ]
    return gathered, low


def local(source_fields, detector_fields, measured, valid_pair, weight_class, absorption):
    cols = absorption.shape[0]
    voxels = cols * 32
    own_rows, own_cols = measured.shape
    pred_scale = 1.0 / jnp.sqrt(jnp.float32(voxels))
    grad_scale = jnp.sqrt(jnp.float32(voxels)) / (jnp.float32(NS) * jnp.float32(ND))
    maskf = valid_pair.astype(jnp.float32) / (1.0 + weight_class.astype(jnp.float32))

    aligned = lax.axis_index("z_mid") == lax.axis_index("z_hi")
    sources, low = gather_sources(source_fields, aligned, lax.axis_index("z_mid") == 0)
    detectors = [detector_fields, lax.ppermute(detector_fields, "z_mid", SWAP)]
    mu_now = [absorption, lax.ppermute(absorption, "z_mid", SWAP)]

    weighted = None
    for step in range(ITERS):
        partial_pred = 0.0
        for s, d, mu in zip(sources, detectors, mu_now):
            scaled = (d * mu[None, :]).astype(BF16)
            partial_pred = partial_pred + lax.dot_general(
                s, scaled, (((1,), (1,)), ((), ())), preferred_element_type=jnp.float32
            )
        sent = partial_pred.astype(BF16).reshape(16, own_rows, own_cols)
        got = lax.all_to_all(sent, SUM, 0, 0)
        predicted = jnp.sum(got.astype(jnp.float32), axis=0)
        weighted = maskf * (predicted * pred_scale - measured)
        weighted_b = weighted.astype(BF16)
        all_weighted = everywhere(weighted_b, SUM, 16).reshape(16 * own_rows, own_cols)
        terms = [
            jnp.sum(jnp.dot(all_weighted, d, preferred_element_type=jnp.float32) * s, axis=0)
            for s, d in zip(sources, detectors)
        ]
        terms = jnp.concatenate(ordered(low, *terms))[None]
        total = jnp.sum(lax.all_gather(terms, "core", axis=0), axis=0)
        if step < ITERS - 1:
            total = jnp.sum(everywhere(total, REST, 16), axis=0)[0]
            gradient = ordered(low, total[:cols], total[cols:])
        else:
            total = jnp.broadcast_to(total.reshape(2, 1, cols), (2, 8, cols))
            total = lax.all_to_all(total.reshape(16, 1, cols), REST, 0, 0)
            gradient = [jnp.sum(total, axis=0).reshape(cols)]
        mu_now = [jnp.maximum(mu - 2.0 * (g * grad_scale), 0.0) for mu, g in zip(mu_now, gradient)]
    return (mu_now[0], weighted)


def solution(mesh):
    fine = Mesh(mesh.devices.reshape(2, 2, 8, 2, 4, 2), AXES)
    placed = (P(OPT, VOX), P(OPT, VOX), P(VOX, OPT), P(VOX, OPT), P(VOX, OPT), P(VOX))
    return jax.shard_map(
        local, mesh=fine, in_specs=placed, out_specs=(P(VOX), P(VOX, OPT)), check_vma=False
    )
```
